32 devices in a mesh: dp: 8 (over z, y), seq: 4 (over x, core).
Axes of the slice: x: 2, y: 2, z: 4, core: 2. Of those that a mesh axis runs over, the one named last changes fastest.
Arguments:
- section_input: bfloat16 [8, 512, 1536], P('dp', 'seq'), may hold values from -6 to 6
- lengths: int32 [8], P('dp'), may hold values from 128 to 512
- depthwise_taps_matrix: float32 [5, 1536], replicated, may hold values from -2.5 to 2.5
- depth_bias: float32 [1536], replicated, may hold values from -3 to 3
- norm_gain: float32 [1536], replicated, may hold values from 0.5 to 1.5
- proj_weight: bfloat16 [768, 1536], replicated, may hold values from -0.15625 to 0.15625
- proj_cotangent: bfloat16 [8, 512, 768], P('dp', 'seq'), may hold values from -6 to 6
- skip_cotangent: bfloat16 [8, 512, 1536], P('dp', 'seq'), may hold values from -6 to 6
Outputs:
- input_grad: bfloat16 [8, 512, 1536], P('dp', 'seq')
- proj_grad: float32 [768, 1536], P('dp', 'seq')
- kernel_grad: float32 [5, 1536], replicated
- bias_grad: float32 [1536], replicated
- gain_grad: float32 [1536], replicated
The draws below stay inside these ranges and needn't reach their ends.
All inputs are finite; a program needn't handle non-finite values.
Results may differ from the reference program's by a relative error of at most 0.0055.
Values may be sent and summed in bfloat16 or wider, within the bound.
No kernel may reach another device: no remote copies, remote signals or barrier semaphores. Data moves between devices by JAX's collectives and lax.ppermute only.
A program may use at most 64 MiB of HBM per device.

```python
import jax
import jax.numpy as jnp
from jax import lax

C = 1536
C2 = 768
K = 5
DILATION_STEP = 4
NPOS = 512
SAMPLES = 8


def place_ends(entries, own_key, low, high):
    longest = entries.shape.index(max(entries.shape))
    spots = []
    for shift in (0, 1):
        where = [jax.random.randint(jax.random.fold_in(own_key, axis), (), 0, length) for axis, length in enumerate(entries.shape)]
        where[longest] = (where[longest] + shift) % entries.shape[longest]
        spots.append(tuple(where))
    return entries.at[spots[0]].set(low).at[spots[1]].set(high)


def strengthened(entries, stream_key, source, target, blocks, factor):
    owner, partner = [(jnp.arange(entries.shape[dim]) // (entries.shape[dim] // blocks)).reshape([-1 if axis == dim else 1 for axis in range(entries.ndim)]) for dim in (source, target)]
    chosen = jax.random.permutation(stream_key, blocks)[partner]
    strong = (owner == chosen) | (owner == (partner + blocks // 2) % blocks)
    return jnp.where(strong, factor * entries, entries)


def levels(rng, extent, shards, smallest, high):
    level = 1.0
    for dim, shards_of in shards:
        draws = jax.random.uniform(jax.random.fold_in(jax.random.fold_in(rng, 6), dim), (shards_of,), jnp.float32, smallest / len(shards), high / len(shards))
        level = level * jnp.repeat(jnp.exp(draws), extent[dim] // shards_of).reshape((-1,) + (1,) * (len(extent) - 1 - dim))
    return level


def noise(stream_key, extent, spread, limit, cuts=(), held_as=jnp.bfloat16):
    values = jax.random.normal(stream_key, extent, jnp.float32) * spread
    if len(cuts) > 0:
        values = levels(stream_key, extent, cuts, -0.22, 0.18) * values
    return jnp.clip(values, min=-limit, max=limit).astype(held_as)


def heavy_noise(rng, extent, deviation, bound, split, heavy, held_as=jnp.bfloat16):
    result = deviation * jax.random.normal(rng, extent, jnp.float32)
    if split:
        result = result * levels(rng, extent, split, -0.22, 0.18)
    return jnp.clip(strengthened(result, jax.random.fold_in(rng, 3), *heavy), -bound, bound).astype(held_as)


def setup_inputs(seed: int = 0) -> dict:
    key_list = jax.random.split(jax.random.key(seed), 9)
    return {
        "section_input": noise(key_list[0], (SAMPLES, NPOS, C), 1.0, 6.0, ((0, 8), (1, 4))),
        "lengths": place_ends(jax.random.randint(key_list[1], (SAMPLES,), NPOS // 4, NPOS + 1), jax.random.fold_in(key_list[1], 1), NPOS // 4, NPOS).astype(jnp.int32),
        "depthwise_taps_matrix": noise(key_list[2], (K, C), K ** -0.5, 2.5, (), jnp.float32),
        "depth_bias": noise(key_list[3], (C,), 0.5, 3.0, (), jnp.float32),
        "norm_gain": jnp.clip(1.0 + 0.1 * jax.random.normal(key_list[4], (C,), jnp.float32), 0.5, 1.5),
        "proj_weight": noise(key_list[5], (C2, C), C ** -0.5, 0.15625),
        "proj_cotangent": heavy_noise(key_list[6], (SAMPLES, NPOS, C2), 1.0, 6.0, ((0, 8), (1, 4)), (0, 2, 8, 2.0)),
        "skip_cotangent": noise(key_list[7], (SAMPLES, NPOS, C), 1.0, 6.0, ((0, 8), (1, 4))),
    }


def norm_gelu(hidden_state, norm_gain):
    inverse = lax.rsqrt(lax.optimization_barrier(jnp.mean(hidden_state * hidden_state, axis=-1, keepdims=True)) + 1e-06)
    return jax.nn.gelu(hidden_state * inverse * norm_gain)

def reference(section_input, lengths, depthwise_taps_matrix, depth_bias, norm_gain, proj_weight, proj_cotangent, skip_cotangent):
    samples = section_input.shape[0]
    position_total = section_input.shape[1]
    channels = section_input.shape[2]
    outputs = proj_cotangent.shape[2]
    kernel_taps = depthwise_taps_matrix.shape[0]
    receptive_reach = kernel_taps // 2 * DILATION_STEP
    positions = jnp.arange(position_total, dtype=jnp.int32)

    def one_sample(carry, item):
        sample_in, length, sample_cot, sample_skip = item
        keep = (positions < length).astype(jnp.bfloat16)[:, None]
        masked = sample_in * keep
        padded_input = jnp.pad(masked.astype(jnp.float32), ((receptive_reach, receptive_reach), (0, 0)))
        hidden_state = jnp.zeros((position_total, channels), jnp.float32) + depth_bias
        for kernel_tap in range(kernel_taps):
            hidden_state = hidden_state + depthwise_taps_matrix[kernel_tap] * padded_input[kernel_tap * DILATION_STEP:kernel_tap * DILATION_STEP + position_total]
        activ, pull = jax.vjp(norm_gelu, hidden_state, norm_gain)
        activ_b = activ.astype(jnp.bfloat16)
        back = jnp.dot(sample_cot, proj_weight, preferred_element_type=jnp.float32) + sample_skip.astype(jnp.float32)
        hidden_grad, gain_part = pull(back)
        grad_b = hidden_grad.astype(jnp.bfloat16)
        gradient_function = grad_b.astype(jnp.float32)
        grad_pad = jnp.pad(gradient_function, ((receptive_reach, receptive_reach), (0, 0)))
        input_grad = jnp.zeros((position_total, channels), jnp.float32)
        for kernel_tap in range(kernel_taps):
            shift_offset = (kernel_taps - 1 - kernel_tap) * DILATION_STEP
            input_grad = input_grad + depthwise_taps_matrix[kernel_tap] * grad_pad[shift_offset:shift_offset + position_total]
        input_grad = (input_grad * keep.astype(jnp.float32)).astype(jnp.bfloat16)
        proj_part = lax.dot_general(sample_cot, activ_b, (((0,), (0,)), ((), ())), preferred_element_type=jnp.float32)
        kernel_partial = jnp.stack([lax.optimization_barrier(jnp.sum(padded_input[kernel_tap * DILATION_STEP:kernel_tap * DILATION_STEP + position_total] * gradient_function, axis=0)) for kernel_tap in range(kernel_taps)])
        bias_part = lax.optimization_barrier(jnp.sum(gradient_function, axis=0))
        proj_sum, kernel_sum, bias_sum, gain_sum = carry
        return ((proj_sum + proj_part, kernel_sum + kernel_partial, bias_sum + bias_part, gain_sum + gain_part), input_grad)
    start = (jnp.zeros((outputs, channels), jnp.float32), jnp.zeros((kernel_taps, channels), jnp.float32), jnp.zeros((channels,), jnp.float32), jnp.zeros((channels,), jnp.float32))
    totals, input_grad = lax.scan(one_sample, start, (section_input, lengths, proj_cotangent, skip_cotangent))
    proj_sum, kernel_sum, bias_sum, gain_sum = totals
    return (input_grad, proj_sum / samples, kernel_sum / samples, bias_sum / samples, gain_sum / samples)
```

```python
import functools

import jax
import jax.numpy as jnp
from jax import lax
from jax.experimental import pallas as pl
from jax.experimental.pallas import tpu as pltpu
from jax.sharding import PartitionSpec as P

DILATION_STEP = 4
LANES = 128
SUBLANES = 8
EPS = 1e-06
GELU_SCALE = 0.7978845608028654
GELU_CUBIC = 0.044715


def padded(cells, sides, width):
    for axis, dim in sides:
        count = lax.axis_size(axis)
        ends = count - 1
        head = lax.slice_in_dim(cells, 0, width, axis=dim)
        tail = lax.slice_in_dim(cells, cells.shape[dim] - width, cells.shape[dim], axis=dim)
        cells = jnp.concatenate(
            [
                lax.ppermute(tail, axis, [(i, (i + 1) % count) for i in range(ends)]),
                cells,
                lax.ppermute(head, axis, [((i + 1) % count, i) for i in range(ends)]),
            ],
            axis=dim,
        )
    return cells


def norm_gelu(hidden_state, norm_gain):
    inverse = lax.rsqrt(jnp.mean(hidden_state * hidden_state, axis=-1, keepdims=True) + EPS)
    return jax.nn.gelu(hidden_state * inverse * norm_gain)


def general_shards(
    section_input,
    lengths,
    depthwise_taps_matrix,
    depth_bias,
    norm_gain,
    proj_weight,
    proj_cotangent,
    skip_cotangent,
):
    samp_count = section_input.shape[0]
    position_count = section_input.shape[1]
    channels = section_input.shape[2]
    outputs = proj_cotangent.shape[2]
    kernel_taps = depthwise_taps_matrix.shape[0]
    receptive_reach = kernel_taps // 2 * DILATION_STEP
    positions = lax.axis_index("seq") * position_count + jnp.arange(position_count, dtype=jnp.int32)
    keep = (positions[None, :] < lengths[:, None]).astype(jnp.bfloat16)[:, :, None]
    masked = section_input * keep
    padded_input = padded(masked, (("seq", 1),), receptive_reach)
    hidden_state = jnp.zeros((samp_count, position_count, channels), jnp.float32) + depth_bias
    for kernel_tap in range(kernel_taps):
        hidden_state = hidden_state + depthwise_taps_matrix[kernel_tap] * padded_input[
            :, kernel_tap * DILATION_STEP : kernel_tap * DILATION_STEP + position_count
        ].astype(jnp.float32)
    activ, pull = jax.vjp(norm_gelu, hidden_state, norm_gain)
    activ_b = activ.astype(jnp.bfloat16)
    cot_rows = proj_cotangent.reshape(samp_count * position_count, outputs)
    back = jnp.dot(cot_rows, proj_weight, preferred_element_type=jnp.float32).reshape(
        samp_count, position_count, channels
    )
    back = back + skip_cotangent.astype(jnp.float32)
    hidden_grad, gain_part = pull(back)
    grad_b = hidden_grad.astype(jnp.bfloat16)
    grad_pad = padded(grad_b, (("seq", 1),), receptive_reach)
    input_grad = jnp.zeros((samp_count, position_count, channels), jnp.float32)
    for kernel_tap in range(kernel_taps):
        shift_offset = (kernel_taps - 1 - kernel_tap) * DILATION_STEP
        input_grad = input_grad + depthwise_taps_matrix[kernel_tap] * grad_pad[
            :, shift_offset : shift_offset + position_count
        ].astype(jnp.float32)
    input_grad = (input_grad * keep.astype(jnp.float32)).astype(jnp.bfloat16)
    gradient_function = grad_b.astype(jnp.float32)
    kernel_partial = jnp.stack(
        [
            jnp.sum(
                padded_input[
                    :, kernel_tap * DILATION_STEP : kernel_tap * DILATION_STEP + position_count
                ].astype(jnp.float32)
                * gradient_function,
                axis=(0, 1),
            )
            for kernel_tap in range(kernel_taps)
        ]
    )
    bias_part = jnp.sum(gradient_function, axis=(0, 1))
    kernel_sum, bias_sum, gain_sum = lax.psum((kernel_partial, bias_part, gain_part), ("dp", "seq"))
    samples_all = samp_count * lax.axis_size("dp")
    activ_cols = lax.all_to_all(activ_b, "seq", split_axis=2, concat_axis=1, tiled=True)
    col_count = activ_cols.shape[2]
    cot_whole = lax.all_gather(proj_cotangent, "seq", axis=1, tiled=True)
    cot_flat = cot_whole.reshape(-1, outputs)
    act_flat = activ_cols.reshape(-1, col_count)
    proj_sum = lax.psum_scatter(
        lax.dot_general(
            cot_flat, act_flat, (((0,), (0,)), ((), ())), preferred_element_type=jnp.float32
        ),
        "dp",
        scatter_dimension=0,
        tiled=True,
    )
    return (
        input_grad,
        proj_sum / samples_all,
        kernel_sum / samples_all,
        bias_sum / samples_all,
        gain_sum / samples_all,
    )


def groups(channels):
    return [slice(start, start + LANES) for start in range(0, channels, LANES)]


def back_kernel(cot_ref, weight_ref, skip_ref, back_ref):
    back_ref[...] = jnp.dot(
        cot_ref[...], weight_ref[...], preferred_element_type=jnp.float32
    ) + skip_ref[...].astype(jnp.float32)


def activ_kernel(
    len_ref, input_ref, left_ref, right_ref, taps_ref, bias_ref, gain_ref, *refs
):
    pad_ref, hidden_ref, inverse_ref, *out_refs, blocks = refs
    rows, channels = input_ref.shape
    reach = left_ref.shape[0]
    taps = taps_ref.shape[0]
    width = blocks.shape[2]
    member = lax.axis_index("seq")
    first = member * rows
    length = len_ref[0]
    place = lax.broadcasted_iota(jnp.int32, (rows + 2 * reach, LANES), 0) + (first - reach)
    keep = place < length
    total = jnp.zeros((rows, LANES), jnp.float32)
    for cols in groups(channels):
        whole = jnp.concatenate(
            [
                left_ref[:, cols].astype(jnp.float32),
                input_ref[:, cols].astype(jnp.float32),
                right_ref[:, cols].astype(jnp.float32),
            ],
            axis=0,
        )
        pad_ref[:, cols] = jnp.where(keep, whole, 0.0)
        hidden = jnp.broadcast_to(bias_ref[:, cols], (rows, LANES))
        for tap in range(taps):
            hidden = hidden + taps_ref[tap : tap + 1, cols] * pad_ref[
                tap * DILATION_STEP : tap * DILATION_STEP + rows, cols
            ]
        hidden_ref[:, cols] = hidden
        total = total + hidden * hidden
    mean = jnp.sum(total, axis=1, keepdims=True) / channels
    inverse = jnp.broadcast_to(lax.rsqrt(mean + EPS), (rows, LANES))
    inverse_ref[...] = inverse
    for cols in groups(channels):
        normed = hidden_ref[:, cols] * inverse * gain_ref[:, cols]
        inner = GELU_SCALE * (normed + GELU_CUBIC * (normed * normed * normed))
        activ = normed * (0.5 * (1.0 + jnp.tanh(inner)))
        block, offset = divmod(cols.start, width)
        blocks[block, :, offset : offset + LANES] = activ.astype(jnp.bfloat16)
    for step, out_ref in enumerate(out_refs):
        out_ref[...] = blocks[member ^ step]


def grad_kernel(
    back_ref, hidden_ref, inverse_ref, pad_ref, gain_ref, grad_ref, head_ref, tail_ref, own_ref, away_ref, scaled_ref, sums_ref
):
    rows, channels = hidden_ref.shape
    reach = head_ref.shape[0]
    taps = 2 * reach // DILATION_STEP + 1
    half = own_ref.shape[1]
    inverse = inverse_ref[...]
    total = jnp.zeros((rows, LANES), jnp.float32)
    sums_ref[...] = jnp.zeros_like(sums_ref)
    for cols in groups(channels):
        hidden = hidden_ref[:, cols]
        gain = gain_ref[:, cols]
        scaled = hidden * inverse
        normed = scaled * gain
        square = normed * normed
        inner = GELU_SCALE * (normed + GELU_CUBIC * (square * normed))
        bend = jnp.tanh(inner)
        slope = 0.5 * (1.0 + bend) + (0.5 * GELU_SCALE) * normed * (1.0 - bend * bend) * (
            1.0 + (3.0 * GELU_CUBIC) * square
        )
        flow = back_ref[:, cols] * slope
        sums_ref[taps + 1 : taps + 2, cols] = jnp.sum(flow * scaled, axis=0, keepdims=True)
        flow = flow * gain
        scaled_ref[:, cols] = flow
        total = total + flow * hidden
    dot = jnp.sum(total, axis=1, keepdims=True) / channels
    pull = jnp.broadcast_to(dot, (rows, LANES)) * inverse * inverse * inverse
    for cols in groups(channels):
        grad = (scaled_ref[:, cols] * inverse - hidden_ref[:, cols] * pull).astype(jnp.bfloat16)
        grad_ref[:, cols] = grad
        head_ref[:, cols] = grad[:reach]
        tail_ref[:, cols] = grad[rows - reach :]
        wide = grad.astype(jnp.float32)
        for tap in range(taps):
            sums_ref[tap : tap + 1, cols] = jnp.sum(
                wide * pad_ref[tap * DILATION_STEP : tap * DILATION_STEP + rows, cols],
                axis=0,
                keepdims=True,
            )
        sums_ref[taps : taps + 1, cols] = jnp.sum(wide, axis=0, keepdims=True)
    core = lax.axis_index("seq") & 1
    own_ref[...] = sums_ref[:, pl.ds(pl.multiple_of(core * half, LANES), half)]
    away_ref[...] = sums_ref[:, pl.ds(pl.multiple_of((1 - core) * half, LANES), half)]


def input_kernel(len_ref, grad_ref, left_ref, right_ref, taps_ref, out_ref, pad_ref):
    rows, channels = grad_ref.shape
    reach = left_ref.shape[0]
    taps = taps_ref.shape[0]
    first = lax.axis_index("seq") * rows
    place = lax.broadcasted_iota(jnp.int32, (rows, LANES), 0) + first
    keep = place < len_ref[0]
    for cols in groups(channels):
        pad_ref[:reach, cols] = left_ref[:, cols].astype(jnp.float32)
        pad_ref[reach : reach + rows, cols] = grad_ref[:, cols].astype(jnp.float32)
        pad_ref[reach + rows :, cols] = right_ref[:, cols].astype(jnp.float32)
        total = jnp.zeros((rows, LANES), jnp.float32)
        for tap in range(taps):
            offset = (taps - 1 - tap) * DILATION_STEP
            total = total + taps_ref[tap : tap + 1, cols] * pad_ref[offset : offset + rows, cols]
        out_ref[:, cols] = jnp.where(keep, total, 0.0).astype(jnp.bfloat16)


def proj_kernel(count, *refs):
    cots, acts = refs[:count], refs[count : 2 * count]
    own_ref, *sent_refs, scratch = refs[2 * count :]
    chunk = own_ref.shape[0]
    cot = jnp.concatenate([ref[...] for ref in cots], axis=0)
    act = jnp.concatenate([ref[...] for ref in acts], axis=0)
    product = lax.dot_general(cot, act, (((0,), (0,)), ((), ())), preferred_element_type=jnp.float32)
    for block in range(scratch.shape[0]):
        scratch[block] = product[block * chunk : (block + 1) * chunk]
    member = lax.axis_index("dp")
    own_ref[...] = scratch[member]
    for step, ref in enumerate(sent_refs, 1):
        ref[...] = scratch[member ^ step].astype(jnp.bfloat16)


def total_kernel(scale, own_ref, *refs):
    *parts, out_ref = refs
    total = own_ref[...]
    for ref in parts:
        total = total + ref[...].astype(jnp.float32)
    out_ref[...] = total / scale


def small_kernel(scale, own_ref, away_ref, kernel_ref, bias_ref, gain_ref, all_ref):
    half = own_ref.shape[1]
    taps = kernel_ref.shape[0]
    core = lax.axis_index("seq") & 1
    all_ref[:, pl.ds(pl.multiple_of(core * half, LANES), half)] = own_ref[...]
    all_ref[:, pl.ds(pl.multiple_of((1 - core) * half, LANES), half)] = away_ref[...]
    kernel_ref[...] = all_ref[:taps, :] / scale
    bias_ref[...] = all_ref[taps : taps + 1, :] / scale
    gain_ref[...] = all_ref[taps + 1 : taps + 2, :] / scale


def vmem(count):
    return [pl.BlockSpec(memory_space=pltpu.VMEM)] * count


def smem():
    return pl.BlockSpec(memory_space=pltpu.SMEM)


def call(kernel, name, in_specs, outs, scratch=()):
    return pl.pallas_call(
        kernel,
        name=name,
        in_specs=in_specs,
        out_shape=[jax.ShapeDtypeStruct(shape, dtype) for shape, dtype in outs],
        out_specs=vmem(len(outs)),
        scratch_shapes=list(scratch),
    )


def flip(value, axis, step):
    return lax.ppermute(value, axis, [(i, i ^ step) for i in range(lax.axis_size(axis))])


def halo(head, tail):
    count = lax.axis_size("seq")
    left = lax.ppermute(tail, "seq", [(i, i + 1) for i in range(count - 1)])
    right = lax.ppermute(head, "seq", [(i + 1, i) for i in range(count - 1)])
    return left, right


def tiled_shards(
    section_input,
    lengths,
    depthwise_taps_matrix,
    depth_bias,
    norm_gain,
    proj_weight,
    proj_cotangent,
    skip_cotangent,
):
    cells, cot, skip = section_input[0], proj_cotangent[0], skip_cotangent[0]
    rows, channels = cells.shape
    outputs = cot.shape[1]
    taps = depthwise_taps_matrix.shape[0]
    reach = taps // 2 * DILATION_STEP
    seq, dp = lax.axis_size("seq"), lax.axis_size("dp")
    width, chunk = channels // seq, outputs // dp
    f32, bf16 = jnp.float32, jnp.bfloat16
    bias, gain = depth_bias[None], norm_gain[None]
    small_rows = -(-(taps + 2) // SUBLANES) * SUBLANES

    left, right = halo(cells[:reach], cells[rows - reach :])
    cots = [cot]
    step = seq // 2
    gathered = {0: cot}
    while step:
        for known in list(gathered):
            gathered[known ^ step] = flip(gathered[known], "seq", step)
        step //= 2
    cots = [gathered[i] for i in range(seq)]

    (back,) = call(back_kernel, "back", vmem(3), [((rows, channels), f32)])(cot, proj_weight, skip)

    pad, hidden, inverse, *acts = call(
        activ_kernel,
        "activ",
        [smem()] + vmem(6),
        [((rows + 2 * reach, channels), f32), ((rows, channels), f32), ((rows, LANES), f32)]
        + [((rows, width), bf16)] * seq,
        [pltpu.VMEM((seq, rows, width), bf16)],
    )(lengths, cells, left, right, depthwise_taps_matrix, bias, gain)
    acts = [acts[0]] + [flip(acts[i], "seq", i) for i in range(1, seq)]

    grad, head, tail, own_sums, away_sums = call(
        grad_kernel,
        "grad",
        vmem(5),
        [((rows, channels), bf16)]
        + [((reach, channels), bf16)] * 2
        + [((small_rows, channels // 2), f32)] * 2,
        [pltpu.VMEM((rows, channels), f32), pltpu.VMEM((small_rows, channels), f32)],
    )(back, hidden, inverse, pad, gain)

    own_proj, *sent = call(
        functools.partial(proj_kernel, seq),
        "proj",
        vmem(2 * seq),
        [((chunk, width), f32)] + [((chunk, width), bf16)] * (dp - 1),
        [pltpu.VMEM((dp, chunk, width), f32)],
    )(*cots, *acts)
    arrived = [flip(part, "dp", i) for i, part in enumerate(sent, 1)]
    samples_all = float(dp)
    (proj_grad,) = call(
        functools.partial(total_kernel, samples_all), "total", vmem(dp), [((chunk, width), f32)]
    )(own_proj, *arrived)

    sums = own_sums + flip(away_sums, "seq", 1)
    step = 1
    while step < dp:
        sums = sums + flip(sums, "dp", step)
        step *= 2
    step = 2
    while step < seq:
        sums = sums + flip(sums, "seq", step)
        step *= 2
    kernel_grad, bias_grad, gain_grad = call(
        functools.partial(small_kernel, samples_all),
        "small",
        vmem(2),
        [((taps, channels), f32), ((1, channels), f32), ((1, channels), f32)],
        [pltpu.VMEM((small_rows, channels), f32)],
    )(sums, flip(sums, "seq", 1))

    grad_left, grad_right = halo(head, tail)
    (input_grad,) = call(
        input_kernel,
        "input",
        [smem()] + vmem(4),
        [((rows, channels), bf16)],
        [pltpu.VMEM((rows + 2 * reach, channels), f32)],
    )(lengths, grad, grad_left, grad_right, depthwise_taps_matrix)
    return input_grad[None], proj_grad, kernel_grad, bias_grad[0], gain_grad[0]


def power_of_two(number):
    return number & (number - 1) == 0


def shards(section_input, lengths, depthwise_taps_matrix, depth_bias, norm_gain, proj_weight, proj_cotangent, skip_cotangent):
    samples, rows, channels = section_input.shape
    outputs = proj_cotangent.shape[2]
    taps = depthwise_taps_matrix.shape[0]
    seq, dp = lax.axis_size("seq"), lax.axis_size("dp")
    tiled = (
        samples == 1
        and rows % (2 * SUBLANES) == 0
        and taps // 2 * DILATION_STEP == SUBLANES
        and seq > 1
        and power_of_two(seq)
        and 1 < dp <= 16
        and power_of_two(dp)
        and channels % (seq * LANES) == 0
        and outputs % (dp * 2 * SUBLANES) == 0
    )
    return (tiled_shards if tiled else general_shards)(
        section_input, lengths, depthwise_taps_matrix, depth_bias, norm_gain, proj_weight, proj_cotangent, skip_cotangent
    )


def solution(mesh):
    in_specs = (
        P("dp", "seq", None),
        P("dp"),
        P(),
        P(),
        P(),
        P(),
        P("dp", "seq", None),
        P("dp", "seq", None),
    )
    out_specs = (P("dp", "seq", None), P("dp", "seq"), P(), P(), P())
    return jax.shard_map(shards, mesh=mesh, in_specs=in_specs, out_specs=out_specs, check_vma=False)
```

```python
import functools

import jax
import jax.numpy as jnp
from jax import lax
from jax.experimental import pallas as pl
from jax.experimental.pallas import tpu as pltpu
from jax.sharding import PartitionSpec as P

DILATION_STEP = 4
LANES = 128
SUBLANES = 8
EPS = 1e-06
GELU_SCALE = 0.7978845608028654
GELU_CUBIC = 0.044715
KERNEL_VMEM = 16 * 2**20
FAR, NEAR = 6, 2
SENT = ((FAR ^ 1,), (1, NEAR ^ 1), (4,), (5,))


def padded(cells, sides, width):
    for axis, dim in sides:
        count = lax.axis_size(axis)
        ends = count - 1
        head = lax.slice_in_dim(cells, 0, width, axis=dim)
        tail = lax.slice_in_dim(cells, cells.shape[dim] - width, cells.shape[dim], axis=dim)
        cells = jnp.concatenate(
            [
                lax.ppermute(tail, axis, [(i, (i + 1) % count) for i in range(ends)]),
                cells,
                lax.ppermute(head, axis, [((i + 1) % count, i) for i in range(ends)]),
            ],
            axis=dim,
        )
    return cells


def norm_gelu(hidden_state, norm_gain):
    inverse = lax.rsqrt(jnp.mean(hidden_state * hidden_state, axis=-1, keepdims=True) + EPS)
    return jax.nn.gelu(hidden_state * inverse * norm_gain)


def general_shards(
    section_input,
    lengths,
    depthwise_taps_matrix,
    depth_bias,
    norm_gain,
    proj_weight,
    proj_cotangent,
    skip_cotangent,
):
    samp_count = section_input.shape[0]
    position_count = section_input.shape[1]
    channels = section_input.shape[2]
    outputs = proj_cotangent.shape[2]
    kernel_taps = depthwise_taps_matrix.shape[0]
    receptive_reach = kernel_taps // 2 * DILATION_STEP
    positions = lax.axis_index("seq") * position_count + jnp.arange(position_count, dtype=jnp.int32)
    keep = (positions[None, :] < lengths[:, None]).astype(jnp.bfloat16)[:, :, None]
    masked = section_input * keep
    padded_input = padded(masked, (("seq", 1),), receptive_reach)
    hidden_state = jnp.zeros((samp_count, position_count, channels), jnp.float32) + depth_bias
    for kernel_tap in range(kernel_taps):
        hidden_state = hidden_state + depthwise_taps_matrix[kernel_tap] * padded_input[
            :, kernel_tap * DILATION_STEP : kernel_tap * DILATION_STEP + position_count
        ].astype(jnp.float32)
    activ, pull = jax.vjp(norm_gelu, hidden_state, norm_gain)
    activ_b = activ.astype(jnp.bfloat16)
    cot_rows = proj_cotangent.reshape(samp_count * position_count, outputs)
    back = jnp.dot(cot_rows, proj_weight, preferred_element_type=jnp.float32).reshape(
        samp_count, position_count, channels
    )
    back = back + skip_cotangent.astype(jnp.float32)
    hidden_grad, gain_part = pull(back)
    grad_b = hidden_grad.astype(jnp.bfloat16)
    grad_pad = padded(grad_b, (("seq", 1),), receptive_reach)
    input_grad = jnp.zeros((samp_count, position_count, channels), jnp.float32)
    for kernel_tap in range(kernel_taps):
        shift_offset = (kernel_taps - 1 - kernel_tap) * DILATION_STEP
        input_grad = input_grad + depthwise_taps_matrix[kernel_tap] * grad_pad[
            :, shift_offset : shift_offset + position_count
        ].astype(jnp.float32)
    input_grad = (input_grad * keep.astype(jnp.float32)).astype(jnp.bfloat16)
    gradient_function = grad_b.astype(jnp.float32)
    kernel_partial = jnp.stack(
        [
            jnp.sum(
                padded_input[
                    :, kernel_tap * DILATION_STEP : kernel_tap * DILATION_STEP + position_count
                ].astype(jnp.float32)
                * gradient_function,
                axis=(0, 1),
            )
            for kernel_tap in range(kernel_taps)
        ]
    )
    bias_part = jnp.sum(gradient_function, axis=(0, 1))
    kernel_sum, bias_sum, gain_sum = lax.psum((kernel_partial, bias_part, gain_part), ("dp", "seq"))
    samples_all = samp_count * lax.axis_size("dp")
    activ_cols = lax.all_to_all(activ_b, "seq", split_axis=2, concat_axis=1, tiled=True)
    col_count = activ_cols.shape[2]
    cot_whole = lax.all_gather(proj_cotangent, "seq", axis=1, tiled=True)
    cot_flat = cot_whole.reshape(-1, outputs)
    act_flat = activ_cols.reshape(-1, col_count)
    proj_sum = lax.psum_scatter(
        lax.dot_general(
            cot_flat, act_flat, (((0,), (0,)), ((), ())), preferred_element_type=jnp.float32
        ),
        "dp",
        scatter_dimension=0,
        tiled=True,
    )
    return (
        input_grad,
        proj_sum / samples_all,
        kernel_sum / samples_all,
        bias_sum / samples_all,
        gain_sum / samples_all,
    )


def groups(channels):
    return [slice(start, start + LANES) for start in range(0, channels, LANES)]


def prep_kernel(taps_hbm, bias_hbm, gain_hbm, cells_hbm, taps_ref, bias_ref, gain_ref, cells_ref, near_ref, far_ref, sems):
    reach = near_ref.shape[0]
    odd = lax.axis_index("seq") & 1
    last = cells_hbm.shape[0] - reach
    near = pl.multiple_of((1 - odd) * last, SUBLANES)
    far = pl.multiple_of(odd * last, SUBLANES)
    pairs = [
        (cells_hbm.at[pl.ds(near, reach)], near_ref),
        (cells_hbm.at[pl.ds(far, reach)], far_ref),
        (cells_hbm, cells_ref),
        (taps_hbm, taps_ref),
        (bias_hbm, bias_ref),
        (gain_hbm, gain_ref),
    ]
    copies = [
        pltpu.make_async_copy(source, target, sems.at[i]) for i, (source, target) in enumerate(pairs)
    ]
    for copy in copies:
        copy.start()
    for copy in copies:
        copy.wait()


def kept_half():
    member = lax.axis_index("seq")
    return (member ^ (member >> 1)) & 1


def sides(odd, near, far):
    return jnp.where(odd, near, far), jnp.where(odd, far, near)


def activ_kernel(
    len_ref, input_ref, near_ref, far_ref, taps_ref, bias_ref, gain_ref, *refs
):
    sources, refs = refs[:3], refs[3:]
    pad_ref, hidden_ref, inverse_ref, *refs, blocks, sems = refs
    loaded, out_refs = refs[:3], refs[3:]
    copies = [
        pltpu.make_async_copy(source, target, sems.at[i])
        for i, (source, target) in enumerate(zip(sources, loaded))
    ]
    for copy in copies:
        copy.start()
    rows, channels = input_ref.shape
    reach = near_ref.shape[0]
    taps = taps_ref.shape[0]
    width = blocks.shape[2]
    member = lax.axis_index("seq")
    odd = (member & 1) == 1
    first = member * rows
    length = len_ref[0]
    place = lax.broadcasted_iota(jnp.int32, (rows + 2 * reach, LANES), 0) + (first - reach)
    keep = place < length
    total = jnp.zeros((rows, LANES), jnp.float32)
    for cols in groups(channels):
        left, right = sides(
            odd, near_ref[:, cols].astype(jnp.float32), far_ref[:, cols].astype(jnp.float32)
        )
        whole = jnp.concatenate([left, input_ref[:, cols].astype(jnp.float32), right], axis=0)
        pad_ref[:, cols] = jnp.where(keep, whole, 0.0)
        hidden = jnp.broadcast_to(bias_ref[cols][None], (rows, LANES))
        for tap in range(taps):
            hidden = hidden + taps_ref[tap : tap + 1, cols] * pad_ref[
                tap * DILATION_STEP : tap * DILATION_STEP + rows, cols
            ]
        hidden_ref[:, cols] = hidden
        total = total + hidden * hidden
    mean = jnp.sum(total, axis=1, keepdims=True) / channels
    inverse = jnp.broadcast_to(lax.rsqrt(mean + EPS), (rows, LANES))
    inverse_ref[...] = inverse
    for cols in groups(channels):
        normed = hidden_ref[:, cols] * inverse * gain_ref[cols][None]
        inner = GELU_SCALE * (normed + GELU_CUBIC * (normed * normed * normed))
        activ = normed * (0.5 * (1.0 + jnp.tanh(inner)))
        block, offset = divmod(cols.start, width)
        blocks[block, :, offset : offset + LANES] = activ.astype(jnp.bfloat16)
    for step, out_ref in enumerate(out_refs):
        out_ref[...] = blocks[member ^ step]
    for copy in copies:
        copy.wait()


def grad_kernel(
    cot_ref, weight_ref, skip_ref, hidden_ref, inverse_ref, pad_ref, gain_ref, grad_ref, near_ref, far_ref, own_ref, away_ref, back_ref, scaled_ref, sums_ref
):
    rows, channels = hidden_ref.shape
    reach = near_ref.shape[0]
    taps = 2 * reach // DILATION_STEP + 1
    half = own_ref.shape[1]
    odd = (lax.axis_index("seq") & 1) == 1
    kept = kept_half()
    inverse = inverse_ref[...]
    back_ref[...] = jnp.dot(cot_ref[...], weight_ref[...], preferred_element_type=jnp.float32)
    total = jnp.zeros((rows, LANES), jnp.float32)
    sums_ref[...] = jnp.zeros_like(sums_ref)
    for cols in groups(channels):
        hidden = hidden_ref[:, cols]
        gain = gain_ref[cols][None]
        scaled = hidden * inverse
        normed = scaled * gain
        square = normed * normed
        inner = GELU_SCALE * (normed + GELU_CUBIC * (square * normed))
        bend = jnp.tanh(inner)
        slope = 0.5 * (1.0 + bend) + (0.5 * GELU_SCALE) * normed * (1.0 - bend * bend) * (
            1.0 + (3.0 * GELU_CUBIC) * square
        )
        flow = (back_ref[:, cols] + skip_ref[:, cols].astype(jnp.float32)) * slope
        sums_ref[taps + 1 : taps + 2, cols] = jnp.sum(flow * scaled, axis=0, keepdims=True)
        flow = flow * gain
        scaled_ref[:, cols] = flow
        total = total + flow * hidden
    dot = jnp.sum(total, axis=1, keepdims=True) / channels
    pull = jnp.broadcast_to(dot, (rows, LANES)) * inverse * inverse * inverse
    for cols in groups(channels):
        grad = (scaled_ref[:, cols] * inverse - hidden_ref[:, cols] * pull).astype(jnp.bfloat16)
        grad_ref[:, cols] = grad
        wide = grad.astype(jnp.float32)
        head, tail = wide[:reach], wide[rows - reach :]
        near_ref[:, cols] = jnp.where(odd, head, tail).astype(jnp.bfloat16)
        far_ref[:, cols] = jnp.where(odd, tail, head).astype(jnp.bfloat16)
        for tap in range(taps):
            sums_ref[tap : tap + 1, cols] = jnp.sum(
                wide * pad_ref[tap * DILATION_STEP : tap * DILATION_STEP + rows, cols],
                axis=0,
                keepdims=True,
            )
        sums_ref[taps : taps + 1, cols] = jnp.sum(wide, axis=0, keepdims=True)
    own_ref[...] = sums_ref[:, pl.ds(pl.multiple_of(kept * half, LANES), half)]
    away_ref[...] = sums_ref[:, pl.ds(pl.multiple_of((1 - kept) * half, LANES), half)]


def input_kernel(len_ref, grad_ref, near_ref, far_ref, taps_ref, out_ref, pad_ref):
    rows, channels = grad_ref.shape
    reach = near_ref.shape[0]
    taps = taps_ref.shape[0]
    member = lax.axis_index("seq")
    odd = (member & 1) == 1
    first = member * rows
    place = lax.broadcasted_iota(jnp.int32, (rows, LANES), 0) + first
    keep = place < len_ref[0]
    for cols in groups(channels):
        left, right = sides(
            odd, near_ref[:, cols].astype(jnp.float32), far_ref[:, cols].astype(jnp.float32)
        )
        pad_ref[:reach, cols] = left
        pad_ref[reach : reach + rows, cols] = grad_ref[:, cols].astype(jnp.float32)
        pad_ref[reach + rows :, cols] = right
        total = jnp.zeros((rows, LANES), jnp.float32)
        for tap in range(taps):
            shift = (taps - 1 - tap) * DILATION_STEP
            total = total + taps_ref[tap : tap + 1, cols] * pad_ref[shift : shift + rows, cols]
        out_ref[:, cols] = jnp.where(keep, total, 0.0).astype(jnp.bfloat16)


def proj_kernel(count, *refs):
    cots, acts = refs[:count], refs[count : 2 * count]
    own_ref, far_ref, near_ref, *sent_refs, scratch = refs[2 * count :]
    chunk = own_ref.shape[0]
    cot = jnp.concatenate([ref[...] for ref in cots], axis=0)
    act = jnp.concatenate([ref[...] for ref in acts], axis=0)
    product = lax.dot_general(cot, act, (((0,), (0,)), ((), ())), preferred_element_type=jnp.float32)
    for block in range(scratch.shape[0]):
        scratch[block] = product[block * chunk : (block + 1) * chunk]
    member = lax.axis_index("dp")
    own_ref[...] = scratch[member]
    far_ref[...] = scratch[member ^ FAR]
    near_ref[...] = scratch[member ^ NEAR]
    for ref, steps in zip(sent_refs, SENT):
        for place, step in enumerate(steps):
            ref[place * chunk : (place + 1) * chunk] = scratch[member ^ step].astype(jnp.bfloat16)


def add_kernel(start, held_ref, arrived_ref, out_ref):
    rows = held_ref.shape[0]
    total = held_ref[...] + arrived_ref[start : start + rows].astype(jnp.float32)
    out_ref[...] = total.astype(jnp.bfloat16)


def write_sums(sums, row, out_ref):
    small, width = sums.shape[0], out_ref.shape[1]
    strips = []
    for start in range(0, sums.shape[1], width):
        value = sums[:, start : start + width]
        high = value.astype(jnp.bfloat16).astype(jnp.float32)
        low = (value - high).astype(jnp.bfloat16).astype(jnp.float32)
        out_ref[row : row + 2 * small] = jnp.concatenate([high, low], axis=0).astype(jnp.bfloat16)
        row += 2 * small
        strips.append(high + low)
    return jnp.concatenate(strips, axis=1)


def read_sums(ref, row, small):
    strips = []
    while row < ref.shape[0]:
        both = ref[row : row + 2 * small].astype(jnp.float32)
        strips.append(both[:small] + both[small:])
        row += 2 * small
    return jnp.concatenate(strips, axis=1)


def pack_kernel(part_ref, sums_ref, out_ref, exact_ref):
    chunk = part_ref.shape[0]
    out_ref[:chunk] = part_ref[...]
    exact_ref[...] = write_sums(sums_ref[...], chunk, out_ref)


def unpack_kernel(chunk, sums_ref, carrier_ref, out_ref):
    out_ref[...] = sums_ref[...] + read_sums(carrier_ref, chunk, sums_ref.shape[0])


def finish_kernel(scale, count, *refs):
    own_ref, *parts = refs[:count]
    kept_ref, opposite_ref, core_ref, cross_ref = refs[count : count + 4]
    proj_ref, kernel_ref, bias_ref, gain_ref, all_ref = refs[count + 4 :]
    total = own_ref[...]
    for ref in parts:
        total = total + ref[: own_ref.shape[0]].astype(jnp.float32)
    proj_ref[...] = total / scale
    half = kept_ref.shape[1]
    taps = kernel_ref.shape[0]
    kept = kept_half()
    all_ref[:, pl.ds(pl.multiple_of(kept * half, LANES), half)] = kept_ref[...] + opposite_ref[...]
    all_ref[:, pl.ds(pl.multiple_of((1 - kept) * half, LANES), half)] = core_ref[...] + cross_ref[...]
    kernel_ref[...] = all_ref[:taps, :] / scale
    for cols in groups(2 * half):
        bias_ref[cols] = all_ref[taps, cols] / scale
        gain_ref[cols] = all_ref[taps + 1, cols] / scale


def call(kernel, args, outs, scratch=(), kept=True, loads=0):
    specs, placed = [], []
    for place, arg in enumerate(args):
        if place >= len(args) - loads:
            specs.append(pl.BlockSpec(memory_space=pl.ANY))
            placed.append(pltpu.with_memory_space_constraint(arg, pltpu.HBM))
        elif arg.dtype == jnp.int32:
            specs.append(pl.BlockSpec(memory_space=pltpu.SMEM))
            placed.append(arg)
        else:
            specs.append(pl.BlockSpec(memory_space=pltpu.VMEM))
            placed.append(pltpu.with_memory_space_constraint(arg, pltpu.VMEM))
    make = pltpu.VMEM if kept else jax.ShapeDtypeStruct
    return pl.pallas_call(
        kernel,
        in_specs=specs,
        out_shape=[make(shape, dtype) for shape, dtype in outs],
        out_specs=[pl.BlockSpec(memory_space=pltpu.VMEM)] * len(outs),
        scratch_shapes=list(scratch),
        compiler_params=pltpu.CompilerParams(vmem_limit_bytes=KERNEL_VMEM),
    )(*placed)


def flip(value, axis, step):
    return lax.ppermute(value, axis, [(i, i ^ step) for i in range(lax.axis_size(axis))])


def exchange(near, far):
    count = lax.axis_size("seq")
    pairs = [(i, i + 1) for i in range(1, count - 1, 2)]
    far = lax.ppermute(far, "seq", pairs + [(j, i) for i, j in pairs])
    return flip(near, "seq", 1), far


def tiled_shards(
    section_input,
    lengths,
    depthwise_taps_matrix,
    depth_bias,
    norm_gain,
    proj_weight,
    proj_cotangent,
    skip_cotangent,
):
    cells, cot, skip = section_input[0], proj_cotangent[0], skip_cotangent[0]
    rows, channels = cells.shape
    outputs = cot.shape[1]
    taps = depthwise_taps_matrix.shape[0]
    reach = taps // 2 * DILATION_STEP
    seq, dp = lax.axis_size("seq"), lax.axis_size("dp")
    width, chunk = channels // seq, outputs // dp
    f32, bf16 = jnp.float32, jnp.bfloat16
    small_rows = -(-(taps + 2) // SUBLANES) * SUBLANES
    samples_all = float(dp)

    taps_kept, bias, gain, cells, near, far = call(
        prep_kernel,
        [depthwise_taps_matrix, depth_bias, norm_gain, cells],
        [((taps, channels), f32), ((channels,), f32), ((channels,), f32)]
        + [((rows, channels), bf16)]
        + [((reach, channels), bf16)] * 2,
        [pltpu.SemaphoreType.DMA((6,))],
        loads=4,
    )
    near, far = exchange(near, far)
    step = seq // 2
    gathered = {0: cot}
    while step:
        for known in list(gathered):
            gathered[known ^ step] = flip(gathered[known], "seq", step)
        step //= 2

    pad, hidden, inverse, weight, skip, near_cot, *acts = call(
        activ_kernel,
        [lengths, cells, near, far, taps_kept, bias, gain, proj_weight, skip, cot],
        [((rows + 2 * reach, channels), f32), ((rows, channels), f32), ((rows, LANES), f32)]
        + [((outputs, channels), bf16), ((rows, channels), bf16), ((rows, outputs), bf16)]
        + [((rows, width), bf16)] * seq,
        [pltpu.VMEM((seq, rows, width), bf16), pltpu.SemaphoreType.DMA((3,))],
        loads=3,
    )
    acts = [acts[0]] + [flip(acts[i], "seq", i) for i in range(1, seq)]

    grad, near, far, own_sums, away_sums = call(
        grad_kernel,
        [near_cot, weight, skip, hidden, inverse, pad, gain],
        [((rows, channels), bf16)]
        + [((reach, channels), bf16)] * 2
        + [((small_rows, channels // 2), f32)] * 2,
        [pltpu.VMEM((rows, channels), f32)] * 2 + [pltpu.VMEM((small_rows, channels), f32)],
    )

    own_proj, held_far, held_near, *sent = call(
        functools.partial(proj_kernel, seq),
        [near_cot] + [gathered[i] for i in range(1, seq)] + acts,
        [((chunk, width), f32)] * 3 + [((len(steps) * chunk, width), bf16) for steps in SENT],
        [pltpu.VMEM((dp, chunk, width), f32)],
    )
    sums = own_sums + flip(away_sums, "seq", 1)
    others = [flip(sums, "dp", step) for step in (1, NEAR, NEAR ^ 1)]
    sums = (sums + others[0]) + (others[1] + others[2])
    half_width = channels // 2
    packed = ((chunk + 2 * small_rows * (half_width // width), width), bf16)
    half_sums = ((small_rows, half_width), f32)

    across_far, across_near, carrier, direct = sent
    direct = flip(direct, "dp", 5)
    across_far = flip(across_far, "dp", 1)
    across_near = flip(across_near, "dp", 1)
    carrier, sums = call(pack_kernel, [carrier, sums], [packed, half_sums])
    carrier = flip(carrier, "dp", 4)
    relayed = []
    for step, held, arrived, start in ((FAR, held_far, across_far, 0), (NEAR, held_near, across_near, chunk)):
        (total,) = call(functools.partial(add_kernel, start), [held, arrived], [((chunk, width), bf16)])
        relayed.append(flip(total, "dp", step))
    (sums,) = call(functools.partial(unpack_kernel, chunk), [sums, carrier], [half_sums])
    terms = [own_proj, across_near, carrier, direct, *relayed]
    proj_grad, kernel_grad, bias_grad, gain_grad = call(
        functools.partial(finish_kernel, samples_all, len(terms)),
        terms + [sums] + [flip(sums, "seq", step) for step in (3, 1, 2)],
        [((chunk, width), f32), ((taps, channels), f32), ((channels,), f32), ((channels,), f32)],
        [pltpu.VMEM((small_rows, channels), f32)],
        kept=False,
    )

    near, far = exchange(near, far)
    (input_grad,) = call(
        input_kernel,
        [lengths, grad, near, far, taps_kept],
        [((rows, channels), bf16)],
        [pltpu.VMEM((rows + 2 * reach, channels), f32)],
        kept=False,
    )
    return input_grad[None], proj_grad, kernel_grad, bias_grad, gain_grad


def shards(section_input, lengths, depthwise_taps_matrix, depth_bias, norm_gain, proj_weight, proj_cotangent, skip_cotangent):
    samples, rows, channels = section_input.shape
    outputs = proj_cotangent.shape[2]
    taps = depthwise_taps_matrix.shape[0]
    seq, dp = lax.axis_size("seq"), lax.axis_size("dp")
    tiled = (
        samples == 1
        and rows % (2 * SUBLANES) == 0
        and taps // 2 * DILATION_STEP == SUBLANES
        and seq == 4
        and dp == 8
        and channels % (seq * LANES) == 0
        and outputs % (dp * 2 * SUBLANES) == 0
    )
    args = (section_input, lengths, depthwise_taps_matrix, depth_bias, norm_gain, proj_weight, proj_cotangent, skip_cotangent)
    if not tiled:
        return general_shards(*args)
    return tiled_shards(*args)


def solution(mesh):
    in_specs = (
        P("dp", "seq", None),
        P("dp"),
        P(),
        P(),
        P(),
        P(),
        P("dp", "seq", None),
        P("dp", "seq", None),
    )
    out_specs = (P("dp", "seq", None), P("dp", "seq"), P(), P(), P())
    return jax.shard_map(shards, mesh=mesh, in_specs=in_specs, out_specs=out_specs, check_vma=False)
```

```python
import functools

import jax
import jax.numpy as jnp
from jax import lax
from jax.experimental import pallas as pl
from jax.experimental.pallas import tpu as pltpu
from jax.sharding import PartitionSpec as P

DILATION_STEP = 4
LANES = 128
SUBLANES = 8
EPS = 1e-06
GELU_SCALE = 0.7978845608028654
GELU_CUBIC = 0.044715
KERNEL_VMEM = 16 * 2**20
FAR, NEAR = 6, 2
SENT = ((FAR ^ 1,), (1, NEAR ^ 1), (4,), (5,))


def padded(cells, sides, width):
    for axis, dim in sides:
        count = lax.axis_size(axis)
        ends = count - 1
        head = lax.slice_in_dim(cells, 0, width, axis=dim)
        tail = lax.slice_in_dim(cells, cells.shape[dim] - width, cells.shape[dim], axis=dim)
        cells = jnp.concatenate(
            [
                lax.ppermute(tail, axis, [(i, (i + 1) % count) for i in range(ends)]),
                cells,
                lax.ppermute(head, axis, [((i + 1) % count, i) for i in range(ends)]),
            ],
            axis=dim,
        )
    return cells


def norm_gelu(hidden_state, norm_gain):
    inverse = lax.rsqrt(jnp.mean(hidden_state * hidden_state, axis=-1, keepdims=True) + EPS)
    return jax.nn.gelu(hidden_state * inverse * norm_gain)


def general_shards(
    section_input,
    lengths,
    depthwise_taps_matrix,
    depth_bias,
    norm_gain,
    proj_weight,
    proj_cotangent,
    skip_cotangent,
):
    samp_count = section_input.shape[0]
    position_count = section_input.shape[1]
    channels = section_input.shape[2]
    outputs = proj_cotangent.shape[2]
    kernel_taps = depthwise_taps_matrix.shape[0]
    receptive_reach = kernel_taps // 2 * DILATION_STEP
    positions = lax.axis_index("seq") * position_count + jnp.arange(position_count, dtype=jnp.int32)
    keep = (positions[None, :] < lengths[:, None]).astype(jnp.bfloat16)[:, :, None]
    masked = section_input * keep
    padded_input = padded(masked, (("seq", 1),), receptive_reach)
    hidden_state = jnp.zeros((samp_count, position_count, channels), jnp.float32) + depth_bias
    for kernel_tap in range(kernel_taps):
        hidden_state = hidden_state + depthwise_taps_matrix[kernel_tap] * padded_input[
            :, kernel_tap * DILATION_STEP : kernel_tap * DILATION_STEP + position_count
        ].astype(jnp.float32)
    activ, pull = jax.vjp(norm_gelu, hidden_state, norm_gain)
    activ_b = activ.astype(jnp.bfloat16)
    cot_rows = proj_cotangent.reshape(samp_count * position_count, outputs)
    back = jnp.dot(cot_rows, proj_weight, preferred_element_type=jnp.float32).reshape(
        samp_count, position_count, channels
    )
    back = back + skip_cotangent.astype(jnp.float32)
    hidden_grad, gain_part = pull(back)
    grad_b = hidden_grad.astype(jnp.bfloat16)
    grad_pad = padded(grad_b, (("seq", 1),), receptive_reach)
    input_grad = jnp.zeros((samp_count, position_count, channels), jnp.float32)
    for kernel_tap in range(kernel_taps):
        shift_offset = (kernel_taps - 1 - kernel_tap) * DILATION_STEP
        input_grad = input_grad + depthwise_taps_matrix[kernel_tap] * grad_pad[
            :, shift_offset : shift_offset + position_count
        ].astype(jnp.float32)
    input_grad = (input_grad * keep.astype(jnp.float32)).astype(jnp.bfloat16)
    gradient_function = grad_b.astype(jnp.float32)
    kernel_partial = jnp.stack(
        [
            jnp.sum(
                padded_input[
                    :, kernel_tap * DILATION_STEP : kernel_tap * DILATION_STEP + position_count
                ].astype(jnp.float32)
                * gradient_function,
                axis=(0, 1),
            )
            for kernel_tap in range(kernel_taps)
        ]
    )
    bias_part = jnp.sum(gradient_function, axis=(0, 1))
    kernel_sum, bias_sum, gain_sum = lax.psum((kernel_partial, bias_part, gain_part), ("dp", "seq"))
    samples_all = samp_count * lax.axis_size("dp")
    activ_cols = lax.all_to_all(activ_b, "seq", split_axis=2, concat_axis=1, tiled=True)
    col_count = activ_cols.shape[2]
    cot_whole = lax.all_gather(proj_cotangent, "seq", axis=1, tiled=True)
    cot_flat = cot_whole.reshape(-1, outputs)
    act_flat = activ_cols.reshape(-1, col_count)
    proj_sum = lax.psum_scatter(
        lax.dot_general(
            cot_flat, act_flat, (((0,), (0,)), ((), ())), preferred_element_type=jnp.float32
        ),
        "dp",
        scatter_dimension=0,
        tiled=True,
    )
    return (
        input_grad,
        proj_sum / samples_all,
        kernel_sum / samples_all,
        bias_sum / samples_all,
        gain_sum / samples_all,
    )


def groups(channels):
    return [slice(start, start + LANES) for start in range(0, channels, LANES)]


def prep_kernel(taps_hbm, bias_hbm, gain_hbm, cells_hbm, taps_ref, bias_ref, gain_ref, cells_ref, near_ref, far_ref, sems):
    reach = near_ref.shape[0]
    odd = lax.axis_index("seq") & 1
    last = cells_hbm.shape[0] - reach
    near = pl.multiple_of((1 - odd) * last, SUBLANES)
    far = pl.multiple_of(odd * last, SUBLANES)
    pairs = [
        (cells_hbm.at[pl.ds(near, reach)], near_ref),
        (cells_hbm.at[pl.ds(far, reach)], far_ref),
        (cells_hbm, cells_ref),
        (taps_hbm, taps_ref),
        (bias_hbm, bias_ref),
        (gain_hbm, gain_ref),
    ]
    copies = [
        pltpu.make_async_copy(source, target, sems.at[i]) for i, (source, target) in enumerate(pairs)
    ]
    for copy in copies:
        copy.start()
    for copy in copies:
        copy.wait()


def kept_half():
    member = lax.axis_index("seq")
    return (member ^ (member >> 1)) & 1


def sides(odd, near, far):
    return jnp.where(odd, near, far), jnp.where(odd, far, near)


def activ_kernel(
    len_ref, input_ref, near_ref, far_ref, taps_ref, bias_ref, gain_ref, *refs
):
    sources, refs = refs[:3], refs[3:]
    pad_ref, hidden_ref, inverse_ref, *refs, blocks, sems = refs
    loaded, out_refs = refs[:3], refs[3:]
    copies = [
        pltpu.make_async_copy(source, target, sems.at[i])
        for i, (source, target) in enumerate(zip(sources, loaded))
    ]
    for copy in copies:
        copy.start()
    rows, channels = input_ref.shape
    reach = near_ref.shape[0]
    taps = taps_ref.shape[0]
    width = blocks.shape[2]
    member = lax.axis_index("seq")
    odd = (member & 1) == 1
    first = member * rows
    length = len_ref[0]
    place = lax.broadcasted_iota(jnp.int32, (rows + 2 * reach, LANES), 0) + (first - reach)
    keep = place < length
    total = jnp.zeros((rows, LANES), jnp.float32)
    for cols in groups(channels):
        left, right = sides(
            odd, near_ref[:, cols].astype(jnp.float32), far_ref[:, cols].astype(jnp.float32)
        )
        whole = jnp.concatenate([left, input_ref[:, cols].astype(jnp.float32), right], axis=0)
        pad_ref[:, cols] = jnp.where(keep, whole, 0.0)
        hidden = jnp.broadcast_to(bias_ref[cols][None], (rows, LANES))
        for tap in range(taps):
            hidden = hidden + taps_ref[tap : tap + 1, cols] * pad_ref[
                tap * DILATION_STEP : tap * DILATION_STEP + rows, cols
            ]
        hidden_ref[:, cols] = hidden
        total = total + hidden * hidden
    mean = jnp.sum(total, axis=1, keepdims=True) / channels
    inverse = jnp.broadcast_to(lax.rsqrt(mean + EPS), (rows, LANES))
    inverse_ref[...] = inverse
    for cols in groups(channels):
        normed = hidden_ref[:, cols] * inverse * gain_ref[cols][None]
        inner = GELU_SCALE * (normed + GELU_CUBIC * (normed * normed * normed))
        activ = normed * (0.5 * (1.0 + jnp.tanh(inner)))
        block, offset = divmod(cols.start, width)
        blocks[block, :, offset : offset + LANES] = activ.astype(jnp.bfloat16)
    for step, out_ref in enumerate(out_refs):
        out_ref[...] = blocks[member ^ step]
    for copy in copies:
        copy.wait()


def grad_kernel(
    cot_ref, weight_ref, skip_ref, hidden_ref, inverse_ref, pad_ref, gain_ref, grad_ref, near_ref, far_ref, own_ref, away_ref, back_ref, scaled_ref, sums_ref
):
    rows, channels = hidden_ref.shape
    reach = near_ref.shape[0]
    taps = 2 * reach // DILATION_STEP + 1
    half = own_ref.shape[1]
    odd = (lax.axis_index("seq") & 1) == 1
    kept = kept_half()
    inverse = inverse_ref[...]
    back_ref[...] = jnp.dot(cot_ref[...], weight_ref[...], preferred_element_type=jnp.float32)
    total = jnp.zeros((rows, LANES), jnp.float32)
    sums_ref[...] = jnp.zeros_like(sums_ref)
    for cols in groups(channels):
        hidden = hidden_ref[:, cols]
        gain = gain_ref[cols][None]
        scaled = hidden * inverse
        normed = scaled * gain
        square = normed * normed
        inner = GELU_SCALE * (normed + GELU_CUBIC * (square * normed))
        bend = jnp.tanh(inner)
        slope = 0.5 * (1.0 + bend) + (0.5 * GELU_SCALE) * normed * (1.0 - bend * bend) * (
            1.0 + (3.0 * GELU_CUBIC) * square
        )
        flow = (back_ref[:, cols] + skip_ref[:, cols].astype(jnp.float32)) * slope
        sums_ref[taps + 1 : taps + 2, cols] = jnp.sum(flow * scaled, axis=0, keepdims=True)
        flow = flow * gain
        scaled_ref[:, cols] = flow
        total = total + flow * hidden
    dot = jnp.sum(total, axis=1, keepdims=True) / channels
    pull = jnp.broadcast_to(dot, (rows, LANES)) * inverse * inverse * inverse
    for cols in groups(channels):
        grad = (scaled_ref[:, cols] * inverse - hidden_ref[:, cols] * pull).astype(jnp.bfloat16)
        grad_ref[:, cols] = grad
        wide = grad.astype(jnp.float32)
        head, tail = wide[:reach], wide[rows - reach :]
        near_ref[:, cols] = jnp.where(odd, head, tail).astype(jnp.bfloat16)
        far_ref[:, cols] = jnp.where(odd, tail, head).astype(jnp.bfloat16)
        for tap in range(taps):
            sums_ref[tap : tap + 1, cols] = jnp.sum(
                wide * pad_ref[tap * DILATION_STEP : tap * DILATION_STEP + rows, cols],
                axis=0,
                keepdims=True,
            )
        sums_ref[taps : taps + 1, cols] = jnp.sum(wide, axis=0, keepdims=True)
    own_ref[...] = sums_ref[:, pl.ds(pl.multiple_of(kept * half, LANES), half)]
    away_ref[...] = sums_ref[:, pl.ds(pl.multiple_of((1 - kept) * half, LANES), half)]


def taps_over(taps_ref, wide, cols, rows):
    taps = taps_ref.shape[0]
    total = jnp.zeros((rows, LANES), jnp.float32)
    for tap in range(taps):
        shift = (taps - 1 - tap) * DILATION_STEP
        total = total + taps_ref[tap : tap + 1, cols] * wide(shift, rows)
    return total


def inner_kernel(len_ref, grad_ref, taps_ref, out_ref, wide_ref):
    rows, channels = grad_ref.shape
    taps = taps_ref.shape[0]
    reach = taps // 2 * DILATION_STEP
    inner = rows - 2 * reach
    first = lax.axis_index("seq") * rows + reach
    keep = lax.broadcasted_iota(jnp.int32, (inner, LANES), 0) + first < len_ref[0]
    for cols in groups(channels):
        wide_ref[...] = grad_ref[:, cols].astype(jnp.float32)
        total = taps_over(taps_ref, lambda shift, count: wide_ref[shift : shift + count], cols, inner)
        out_ref[:, cols] = jnp.where(keep, total, 0.0).astype(jnp.bfloat16)


def edge_rows(edge_row, len_ref, inner_ref, grad_ref, near_ref, carrier_ref, taps_ref, out_ref, wide_ref):
    rows, channels = grad_ref.shape
    reach = near_ref.shape[0]
    half = carrier_ref.shape[1]
    member = lax.axis_index("seq")
    odd = (member & 1) == 1
    outer = (member == 0) | (member == lax.axis_size("seq") - 1)
    first = member * rows
    place = lax.broadcasted_iota(jnp.int32, (reach, LANES), 0) + first
    out_ref[reach : rows - reach] = inner_ref[...]
    for cols in groups(channels):
        strip, offset = divmod(cols.start, half)
        row = edge_row + strip * reach
        far = carrier_ref[row : row + reach, offset : offset + LANES].astype(jnp.float32)
        left, right = sides(
            odd, near_ref[:, cols].astype(jnp.float32), jnp.where(outer, 0.0, far)
        )
        head = grad_ref[: 2 * reach, cols].astype(jnp.float32)
        tail = grad_ref[rows - 2 * reach :, cols].astype(jnp.float32)
        for side, (start, parts) in enumerate(((0, (left, head)), (rows - reach, (tail, right)))):
            wide_ref[side] = jnp.concatenate(parts, axis=0)
            total = taps_over(
                taps_ref, lambda shift, count: wide_ref[side, shift : shift + count], cols, reach
            )
            total = jnp.where(place + start < len_ref[0], total, 0.0)
            out_ref[start : start + reach, cols] = total.astype(jnp.bfloat16)


def proj_kernel(count, *refs):
    cots, acts = refs[:count], refs[count : 2 * count]
    own_ref, far_ref, near_ref, *sent_refs, scratch = refs[2 * count :]
    chunk = own_ref.shape[0]
    cot = jnp.concatenate([ref[...] for ref in cots], axis=0)
    act = jnp.concatenate([ref[...] for ref in acts], axis=0)
    product = lax.dot_general(cot, act, (((0,), (0,)), ((), ())), preferred_element_type=jnp.float32)
    for block in range(scratch.shape[0]):
        scratch[block] = product[block * chunk : (block + 1) * chunk]
    member = lax.axis_index("dp")
    own_ref[...] = scratch[member]
    far_ref[...] = scratch[member ^ FAR]
    near_ref[...] = scratch[member ^ NEAR]
    for ref, steps in zip(sent_refs, SENT):
        for place, step in enumerate(steps):
            ref[place * chunk : (place + 1) * chunk] = scratch[member ^ step].astype(jnp.bfloat16)


def add_kernel(start, held_ref, arrived_ref, out_ref):
    rows = held_ref.shape[0]
    total = held_ref[...] + arrived_ref[start : start + rows].astype(jnp.float32)
    out_ref[...] = total.astype(jnp.bfloat16)


def write_sums(sums, row, out_ref):
    small, width = sums.shape[0], out_ref.shape[1]
    strips = []
    for start in range(0, sums.shape[1], width):
        value = sums[:, start : start + width]
        high = value.astype(jnp.bfloat16).astype(jnp.float32)
        low = (value - high).astype(jnp.bfloat16).astype(jnp.float32)
        out_ref[row : row + 2 * small] = jnp.concatenate([high, low], axis=0).astype(jnp.bfloat16)
        row += 2 * small
        strips.append(high + low)
    return jnp.concatenate(strips, axis=1)


def read_sums(ref, row, small):
    strips = []
    while row < ref.shape[0]:
        both = ref[row : row + 2 * small].astype(jnp.float32)
        strips.append(both[:small] + both[small:])
        row += 2 * small
    return jnp.concatenate(strips, axis=1)


def pack_kernel(part_ref, sums_ref, out_ref, exact_ref):
    chunk = part_ref.shape[0]
    out_ref[:chunk] = part_ref[...]
    exact_ref[...] = write_sums(sums_ref[...], chunk, out_ref)


def unpack_kernel(chunk, sums_ref, carrier_ref, edge_ref, out_ref, exact_ref):
    small, half = sums_ref.shape
    total = sums_ref[...] + read_sums(carrier_ref, chunk, small)
    exact_ref[...] = write_sums(total, 0, out_ref)
    row = 2 * small
    for start in range(0, edge_ref.shape[1], half):
        out_ref[row : row + edge_ref.shape[0]] = edge_ref[:, start : start + half]
        row += edge_ref.shape[0]


def finish_kernel(scale, count, edge_row, *refs):
    own_ref, *parts = refs[:count]
    kept_ref, opposite_ref, core_ref, cross_ref, *rest = refs[count:]
    *rows_refs, input_ref, proj_ref, kernel_ref, bias_ref, gain_ref, all_ref, wide_ref = rest
    len_ref, inner_ref, grad_ref, near_ref, taps_ref = rows_refs
    edge_rows(
        edge_row, len_ref, inner_ref, grad_ref, near_ref, opposite_ref, taps_ref, input_ref, wide_ref
    )
    total = own_ref[...]
    for ref in parts:
        total = total + ref[: own_ref.shape[0]].astype(jnp.float32)
    proj_ref[...] = total / scale
    small, half = kept_ref.shape
    kept_sum = kept_ref[...] + read_sums(opposite_ref.at[: 2 * small], 0, small)
    taps = kernel_ref.shape[0]
    kept = kept_half()
    all_ref[:, pl.ds(pl.multiple_of(kept * half, LANES), half)] = kept_sum
    all_ref[:, pl.ds(pl.multiple_of((1 - kept) * half, LANES), half)] = core_ref[...] + cross_ref[...]
    kernel_ref[...] = all_ref[:taps, :] / scale
    for cols in groups(2 * half):
        bias_ref[cols] = all_ref[taps, cols] / scale
        gain_ref[cols] = all_ref[taps + 1, cols] / scale


def call(kernel, args, outs, scratch=(), kept=True, loads=0):
    specs, placed = [], []
    for place, arg in enumerate(args):
        if place >= len(args) - loads:
            specs.append(pl.BlockSpec(memory_space=pl.ANY))
            placed.append(pltpu.with_memory_space_constraint(arg, pltpu.HBM))
        elif arg.dtype == jnp.int32:
            specs.append(pl.BlockSpec(memory_space=pltpu.SMEM))
            placed.append(arg)
        else:
            specs.append(pl.BlockSpec(memory_space=pltpu.VMEM))
            placed.append(pltpu.with_memory_space_constraint(arg, pltpu.VMEM))
    make = pltpu.VMEM if kept else jax.ShapeDtypeStruct
    return pl.pallas_call(
        kernel,
        in_specs=specs,
        out_shape=[make(shape, dtype) for shape, dtype in outs],
        out_specs=[pl.BlockSpec(memory_space=pltpu.VMEM)] * len(outs),
        scratch_shapes=list(scratch),
        compiler_params=pltpu.CompilerParams(vmem_limit_bytes=KERNEL_VMEM),
    )(*placed)


def flip(value, axis, step):
    return lax.ppermute(value, axis, [(i, i ^ step) for i in range(lax.axis_size(axis))])


def exchange(near, far):
    count = lax.axis_size("seq")
    pairs = [(i, i + 1) for i in range(1, count - 1, 2)]
    far = lax.ppermute(far, "seq", pairs + [(j, i) for i, j in pairs])
    return flip(near, "seq", 1), far


def tiled_shards(
    section_input,
    lengths,
    depthwise_taps_matrix,
    depth_bias,
    norm_gain,
    proj_weight,
    proj_cotangent,
    skip_cotangent,
):
    cells, cot, skip = section_input[0], proj_cotangent[0], skip_cotangent[0]
    rows, channels = cells.shape
    outputs = cot.shape[1]
    taps = depthwise_taps_matrix.shape[0]
    reach = taps // 2 * DILATION_STEP
    seq, dp = lax.axis_size("seq"), lax.axis_size("dp")
    width, chunk = channels // seq, outputs // dp
    f32, bf16 = jnp.float32, jnp.bfloat16
    small_rows = -(-(taps + 2) // SUBLANES) * SUBLANES
    samples_all = float(dp)

    taps_kept, bias, gain, cells, near, far = call(
        prep_kernel,
        [depthwise_taps_matrix, depth_bias, norm_gain, cells],
        [((taps, channels), f32), ((channels,), f32), ((channels,), f32)]
        + [((rows, channels), bf16)]
        + [((reach, channels), bf16)] * 2,
        [pltpu.SemaphoreType.DMA((6,))],
        loads=4,
    )
    near, far = exchange(near, far)
    step = seq // 2
    gathered = {0: cot}
    while step:
        for known in list(gathered):
            gathered[known ^ step] = flip(gathered[known], "seq", step)
        step //= 2

    pad, hidden, inverse, weight, skip, near_cot, *acts = call(
        activ_kernel,
        [lengths, cells, near, far, taps_kept, bias, gain, proj_weight, skip, cot],
        [((rows + 2 * reach, channels), f32), ((rows, channels), f32), ((rows, LANES), f32)]
        + [((outputs, channels), bf16), ((rows, channels), bf16), ((rows, outputs), bf16)]
        + [((rows, width), bf16)] * seq,
        [pltpu.VMEM((seq, rows, width), bf16), pltpu.SemaphoreType.DMA((3,))],
        loads=3,
    )
    acts = [acts[0]] + [flip(acts[i], "seq", i) for i in range(1, seq)]

    grad, near, far, own_sums, away_sums = call(
        grad_kernel,
        [near_cot, weight, skip, hidden, inverse, pad, gain],
        [((rows, channels), bf16)]
        + [((reach, channels), bf16)] * 2
        + [((small_rows, channels // 2), f32)] * 2,
        [pltpu.VMEM((rows, channels), f32)] * 2 + [pltpu.VMEM((small_rows, channels), f32)],
    )

    own_proj, held_far, held_near, *sent = call(
        functools.partial(proj_kernel, seq),
        [near_cot] + [gathered[i] for i in range(1, seq)] + acts,
        [((chunk, width), f32)] * 3 + [((len(steps) * chunk, width), bf16) for steps in SENT],
        [pltpu.VMEM((dp, chunk, width), f32)],
    )
    sums = own_sums + flip(away_sums, "seq", 1)
    others = [flip(sums, "dp", step) for step in (1, NEAR, NEAR ^ 1)]
    sums = (sums + others[0]) + (others[1] + others[2])
    half_width = channels // 2
    packed = ((chunk + 2 * small_rows * (half_width // width), width), bf16)
    half_sums = ((small_rows, half_width), f32)

    across_far, across_near, carrier, direct = sent
    direct = flip(direct, "dp", 5)
    across_far = flip(across_far, "dp", 1)
    across_near = flip(across_near, "dp", 1)
    carrier, sums = call(pack_kernel, [carrier, sums], [packed, half_sums])
    carrier = flip(carrier, "dp", 4)
    relayed = []
    for step, held, arrived, start in ((FAR, held_far, across_far, 0), (NEAR, held_near, across_near, chunk)):
        (total,) = call(functools.partial(add_kernel, start), [held, arrived], [((chunk, width), bf16)])
        relayed.append(flip(total, "dp", step))
    edge_row = 2 * small_rows
    message, sums = call(
        functools.partial(unpack_kernel, chunk),
        [sums, carrier, far],
        [((edge_row + reach * channels // half_width, half_width), bf16), half_sums],
    )
    message = flip(message, "seq", 3)
    near = flip(near, "seq", 1)
    (inner,) = call(
        inner_kernel,
        [lengths, grad, taps_kept],
        [((rows - 2 * reach, channels), bf16)],
        [pltpu.VMEM((rows, LANES), f32)],
    )
    terms = [own_proj, across_near, carrier, direct, *relayed]
    input_grad, proj_grad, kernel_grad, bias_grad, gain_grad = call(
        functools.partial(finish_kernel, samples_all, len(terms), edge_row),
        terms
        + [sums, message]
        + [flip(sums, "seq", step) for step in (1, 2)]
        + [lengths, inner, grad, near, taps_kept],
        [((rows, channels), bf16), ((chunk, width), f32)]
        + [((taps, channels), f32), ((channels,), f32), ((channels,), f32)],
        [pltpu.VMEM((small_rows, channels), f32), pltpu.VMEM((2, 3 * reach, LANES), f32)],
        kept=False,
    )
    return input_grad[None], proj_grad, kernel_grad, bias_grad, gain_grad


def shards(section_input, lengths, depthwise_taps_matrix, depth_bias, norm_gain, proj_weight, proj_cotangent, skip_cotangent):
    samples, rows, channels = section_input.shape
    outputs = proj_cotangent.shape[2]
    taps = depthwise_taps_matrix.shape[0]
    seq, dp = lax.axis_size("seq"), lax.axis_size("dp")
    tiled = (
        samples == 1
        and rows % (2 * SUBLANES) == 0
        and taps // 2 * DILATION_STEP == SUBLANES
        and seq == 4
        and dp == 8
        and channels % (seq * LANES) == 0
        and outputs % (dp * 2 * SUBLANES) == 0
    )
    args = (section_input, lengths, depthwise_taps_matrix, depth_bias, norm_gain, proj_weight, proj_cotangent, skip_cotangent)
    if not tiled:
        return general_shards(*args)
    return tiled_shards(*args)


def solution(mesh):
    in_specs = (
        P("dp", "seq", None),
        P("dp"),
        P(),
        P(),
        P(),
        P(),
        P("dp", "seq", None),
        P("dp", "seq", None),
    )
    out_specs = (P("dp", "seq", None), P("dp", "seq"), P(), P(), P())
    return jax.shard_map(shards, mesh=mesh, in_specs=in_specs, out_specs=out_specs, check_vma=False)
```
